1024 devices in a mesh: hidden: 16 (over y_lo, z), width: 8 (over x), replica: 8 (over y_hi, core).
Axes of the slice: x: 8, y: 8 (y_hi: 4, y_lo: 2; y = y_hi * 2 + y_lo), z: 8, core: 2. Of those that a mesh axis runs over, the one named last changes fastest.
Arguments:
- saved_input: bfloat16 [2048, 12288], P(('replica', 'hidden'), 'width'), may hold values from -0.75 to 0.75
- grad_out: bfloat16 [2048, 24576], P(('replica', 'width'), 'hidden'), may hold values from -16 to 16
- weight: bfloat16 [12288, 24576], P('width', 'hidden'), may hold values from -0.0546875 to 0.0546875
- samples: int32 [64], replicated, may hold values from 8 to 16
- correct: int32 [64], replicated, may hold values from 0 to 8
- prompt_ids: int32 [2048], P('replica'), may hold values from 0 to 63
Outputs:
- grad_input: bfloat16 [2048, 12288], P(('replica', 'hidden'), 'width')
- grad_weight: float32 [12288, 24576], P(('width', 'replica'), 'hidden')
The draws below stay inside these ranges and needn't reach their ends.
Inputs may be any that keep to these rules, and one draw needn't show every extreme that they name: correct[i] <= samples[i] for every prompt.
All inputs are finite; a program needn't handle non-finite values.
Results may differ from the reference program's by a relative error of at most 0.012.
Values may be sent and summed in bfloat16 or wider, within the bound.
A program may use at most 64 MiB of HBM per device.

```python
import jax
import jax.numpy as jnp
from jax import lax

D = 12288
FF = 24576
TOK_REP = 256
PROMPTS = 64
K = 4
TOKENS = 2048
N_REPLICA = 8


def place_ends(entries, own_key, low, high):
    index_at = [jax.random.randint(jax.random.fold_in(own_key, axis), (), 0, length) for axis, length in enumerate(entries.shape)]
    main_axis = entries.shape.index(max(entries.shape))
    beside = index_at[:main_axis] + [(index_at[main_axis] + 1) % entries.shape[main_axis]] + index_at[main_axis + 1:]
    return entries.at[tuple(index_at)].set(low).at[tuple(beside)].set(high)


def with_spikes(result, own_key, source, target, blocks, factor):
    def block_of(dim):
        return (jnp.arange(result.shape[dim]) // (result.shape[dim] // blocks)).reshape((-1,) + (1,) * (result.ndim - 1 - dim))

    one_side = jax.random.permutation(own_key, blocks)[block_of(target)]
    second = (block_of(target) + blocks // 2) % blocks
    return jnp.where((block_of(source) == one_side) | (block_of(source) == second), factor * result, result)


def block_levels(stream_key, shape, split, least, largest):
    level, own = 1.0, jax.random.fold_in(stream_key, 6)
    for position, parts in split:
        steps = jnp.exp(jax.random.uniform(jax.random.fold_in(own, position), (parts,), jnp.float32, least / len(split), largest / len(split)))
        level = level * jnp.repeat(steps, shape[position] // parts).reshape([-1 if axis == position else 1 for axis in range(len(shape))])
    return level


def noise(key, extent, scale, most, shards=(), kind=jnp.bfloat16):
    gain = block_levels(key, extent, shards, -0.22, 0.18) if shards else 1.0
    drawn = jax.random.normal(key, extent, jnp.float32) * scale * gain
    return jnp.minimum(jnp.maximum(drawn, -most), most).astype(kind)


def bell_draw_with(stream_key, dims, deviation, reach, split, heavy, dtype=jnp.bfloat16):
    values = deviation * jax.random.normal(stream_key, dims, jnp.float32)
    if split:
        values = values * block_levels(stream_key, dims, split, -0.22, 0.18)
    return jnp.clip(with_spikes(values, jax.random.fold_in(stream_key, 3), *heavy), -reach, reach).astype(dtype)


def setup_inputs(seed: int = 0) -> dict:
    seeds = jax.random.split(jax.random.key(seed), 7)
    return {
        "saved_input": bell_draw_with(seeds[0], (TOKENS, D), 0.03, 0.75, ((0, 128), (1, 8)), (0, 1, 128, 5.5)),
        "grad_out": bell_draw_with(seeds[1], (TOKENS, FF), 1.0, 16.0, ((0, 64), (1, 16)), (1, 0, 64, 4.0)),
        "weight": noise(seeds[2], (D, FF), D ** -0.5, 0.0546875, ((0, 8), (1, 16))),
        "samples": place_ends(jax.random.randint(seeds[3], (PROMPTS,), 8, 17), jax.random.fold_in(seeds[3], 1), 8, 16).astype(jnp.int32),
        "correct": place_ends(jax.random.randint(seeds[4], (PROMPTS,), 0, 9), jax.random.fold_in(seeds[4], 1), 0, 8).astype(jnp.int32),
        "prompt_ids": place_ends(jax.random.randint(seeds[5], (TOKENS,), 0, PROMPTS), jax.random.fold_in(seeds[5], 1), 0, PROMPTS - 1).astype(jnp.int32),
    }


def pass_weights(samples, correct):
    total = samples.astype(jnp.float32)
    good = correct.astype(jnp.float32)
    missing = jnp.ones_like(total)
    for factor_index in range(K):
        missing = missing * jnp.maximum(total - good - factor_index, 0.0) / (total - factor_index)
    return 1.0 - missing


def reference(saved_input, grad_out, weight, samples, correct, prompt_ids):
    pass_at_k = pass_weights(samples, correct)
    token_weight = lax.optimization_barrier(pass_at_k[prompt_ids].astype(jnp.bfloat16))
    scaled = (grad_out.astype(jnp.float32) * token_weight.astype(jnp.float32)[:, None]).astype(jnp.bfloat16)
    grad_input = lax.dot_general(scaled, weight, (((1,), (1,)), ((), ())), preferred_element_type=jnp.float32).astype(jnp.bfloat16)
    input_groups = saved_input.reshape(N_REPLICA, TOK_REP, D)
    scaled_groups = scaled.reshape(N_REPLICA, TOK_REP, FF)

    def accumulate(total, pair):
        partial_sum = lax.dot_general(pair[0], pair[1], (((0,), (0,)), ((), ())), preferred_element_type=jnp.float32)
        rounded = lax.optimization_barrier(partial_sum.astype(jnp.bfloat16))
        return total + rounded.astype(jnp.float32), None

    grad_weight, _ = lax.scan(accumulate, jnp.zeros((D, FF), jnp.float32), (input_groups, scaled_groups))
    return grad_input, grad_weight
```

```python
import functools

import jax
import jax.numpy as jnp
from jax import lax
from jax.experimental import pallas as pl
from jax.experimental.pallas import tpu as pltpu
from jax.sharding import PartitionSpec as P

K = 4
MESH = pl.DeviceIdType.MESH
F32 = jnp.float32
BF16 = jnp.bfloat16

NX = 8
NZ = 8
NK = 4
HALF = NX // 2


def pass_weights(samples, correct):
    total = samples.astype(jnp.float32)
    good = correct.astype(jnp.float32)
    missing = jnp.ones_like(total)
    for factor_index in range(K):
        missing = missing * jnp.maximum(total - good - factor_index, 0.0) / (total - factor_index)
    return 1.0 - missing


def token_weights(prompt_ids, samples, correct):
    pass_at_k = pass_weights(samples, correct)
    prompt_range = jnp.arange(samples.shape[0], dtype=jnp.int32)
    matches = prompt_ids[:, None] == prompt_range[None, :]
    picked = jnp.sum(jnp.where(matches, pass_at_k[None, :], 0.0), axis=1)
    rounded = lax.optimization_barrier(picked.astype(jnp.bfloat16))
    return rounded.astype(jnp.float32)


def kernel(
    g_in, x_in, w_hbm, gw_out, gi_out,
    gbuf, xbuf, wv, part, rb1, sb, rb2, acc, xt,
    loc_sem, ring_s, ring_r, cc_s, cc_r, ye_s, ye_r, xa_s, xa_r,
    yl_s, yl_r, zr_s, zr_r, xc_s, xc_r, t1_s, t1_r, t2_s, t2_r,
):
    h = lax.axis_index("hidden")
    w = lax.axis_index("width")
    r = lax.axis_index("replica")
    k, c = r // 2, lax.rem(r, 2)
    yl, z = h // NZ, lax.rem(h, NZ)
    zq, zh = z // 2, lax.rem(z, 2)

    def xdev(d):
        return {"width": lax.rem(w + d + NX, NX)}

    def zdev(d):
        return {"hidden": yl * NZ + lax.rem(z + d + NZ, NZ)}

    def kdev(d):
        return {"replica": lax.rem(k + d, NK) * 2 + c}

    partner = {"replica": k * 2 + 1 - c}
    yldev = {"hidden": (1 - yl) * NZ + z}
    sends = []

    def send(src, dst, ss, rs, dev):
        cp = pltpu.make_async_remote_copy(
            src_ref=src, dst_ref=dst, send_sem=ss, recv_sem=rs, device_id=dev, device_id_type=MESH
        )
        cp.start()
        sends.append(cp)

    def arrived(dst, ss, rs, dev):
        pltpu.make_async_remote_copy(
            src_ref=dst, dst_ref=dst, send_sem=ss, recv_sem=rs, device_id=dev, device_id_type=MESH
        ).wait_recv()

    shift = (0, 1, 3, 2)
    kp = [lax.rem(k + s, NK) for s in shift]

    loads = [
        pltpu.make_async_copy(g_in, gbuf.at[k, w, c], loc_sem.at[0]),
        pltpu.make_async_copy(
            x_in.at[:, pl.ds(pl.multiple_of(k * 384, 384), 384)], xbuf.at[k, yl, zq, c, zh], loc_sem.at[1]
        ),
        pltpu.make_async_copy(w_hbm, wv, loc_sem.at[2]),
    ]
    for cp in loads:
        cp.start()

    bar = pltpu.get_barrier_semaphore()
    for dev in (xdev(1), xdev(-1), zdev(1), zdev(-1), kdev(1), kdev(3), yldev, partner):
        pl.semaphore_signal(bar, inc=1, device_id=dev, device_id_type=MESH)
    pl.semaphore_wait(bar, 8)

    def xa_send(d):
        to = lax.rem(k + d, NK)
        send(
            x_in.at[:, pl.ds(pl.multiple_of(to * 384, 384), 384)],
            xbuf.at[k, yl, zq, c, zh], xa_s.at[d - 1], xa_r.at[d - 1], kdev(d),
        )

    def xa_wait(d):
        frm = lax.rem(k + NK - d, NK)
        arrived(xbuf.at[frm, yl, zq, c, zh], xa_s.at[d - 1], xa_r.at[d - 1], kdev(d))

    def ye_send(d):
        send(g_in, gbuf.at[k, w, c], ye_s.at[d - 1], ye_r.at[d - 1], kdev(d))

    def ye_wait(d):
        frm = lax.rem(k + NK - d, NK)
        arrived(gbuf.at[frm, w, c], ye_s.at[d - 1], ye_r.at[d - 1], kdev(d))

    def blk(p, e, s):
        m = lax.rem(w - e * s + NX, NX)
        ref = gbuf.at[kp[p], m, c]
        return ref.at[0 if e == 1 else 1] if s == HALF else ref

    def fwd_view(p, e, s):
        m = lax.rem(w - e * s + NX, NX)
        ref = gbuf.at[kp[p], m, c]
        return ref.at[0 if e == 1 else 1] if s == HALF - 1 else ref

    def cc_send(p, i, ref, src=None):
        send(ref if src is None else src, ref, cc_s.at[p, i], cc_r.at[p, i], partner)

    def ring_start(p):
        own = gbuf.at[kp[p], w, c]
        src = g_in if p == 0 else own
        for i, e in enumerate((1, -1)):
            send(src, own, ring_s.at[p, i, 0], ring_r.at[p, i, 0], xdev(e))
        cc_send(p, 0, own, src)

    def ring_adv(p, s):
        for i, e in enumerate((1, -1)):
            arrived(blk(p, e, s), ring_s.at[p, i, s - 1], ring_r.at[p, i, s - 1], xdev(e))
            if s < HALF:
                ref = fwd_view(p, e, s)
                send(ref, ref, ring_s.at[p, i, s], ring_r.at[p, i, s], xdev(e))
            cc_send(p, 1 + 2 * (s - 1) + i, blk(p, e, s))

    def cc_wait(p):
        o = 1 - c
        arrived(gbuf.at[kp[p], w, o], cc_s.at[p, 0], cc_r.at[p, 0], partner)
        for s in range(1, HALF + 1):
            for i, e in enumerate((1, -1)):
                m = lax.rem(w - e * s + NX, NX)
                ref = gbuf.at[kp[p], m, o]
                if s == HALF:
                    ref = ref.at[i]
                n = 1 + 2 * (s - 1) + i
                arrived(ref, cc_s.at[p, n], cc_r.at[p, n], partner)

    def zblk(d, last, i):
        zz = lax.rem(z + d + NZ, NZ)
        if last:
            return xbuf.at[:, i, zz // 2, c, lax.rem(zz, 2)]
        return xbuf.at[:, :, zz // 2, c, lax.rem(zz, 2)]

    def z_start():
        for i, e in enumerate((1, -1)):
            ref = zblk(0, False, i)
            send(ref, ref, zr_s.at[i, 0], zr_r.at[i, 0], zdev(e))

    def z_adv(s):
        for i, e in enumerate((1, -1)):
            arrived(zblk(-e * s, s == HALF, i), zr_s.at[i, s - 1], zr_r.at[i, s - 1], zdev(e))
            if s < HALF:
                ref = zblk(-e * s, s == HALF - 1, i)
                send(ref, ref, zr_s.at[i, s], zr_r.at[i, s], zdev(e))

    def t3_dot(n):
        lhs = gbuf[k, :, c].reshape(256, 1536)
        out = lax.dot_general(
            lhs, wv[pl.ds(n * 512, 512), :], (((1,), (1,)), ((), ())), preferred_element_type=F32
        )
        part[:, :, :, pl.ds(n * 512, 512)] = out.astype(BF16).reshape(2, NZ, 16, 512)

    order = (4, 3, 5, 2, 6, 1, 7, 0)

    def t3_send():
        for d in order:
            zz = lax.rem(z + d, NZ)
            send(part.at[1 - yl, zz], rb1.at[d], t1_s.at[d], t1_r.at[d], yldev)

    def t3_pair(d):
        zz = lax.rem(z + d, NZ)
        arrived(rb1.at[d], t1_s.at[d], t1_r.at[d], yldev)
        both = part[yl, zz].astype(F32) + rb1[d].astype(F32)
        sb[d] = both.astype(BF16)

    def t3_out(d):
        if d:
            send(sb.at[d], rb2.at[d], t2_s.at[d], t2_r.at[d], zdev(d))

    def t3_final():
        total = sb[0].astype(F32)
        for d in range(1, NZ):
            arrived(rb2.at[d], t2_s.at[d], t2_r.at[d], zdev(d))
            total = total + rb2[d].astype(F32)
        gi_out[...] = total.astype(BF16)

    win = pl.ds(pl.multiple_of(c * 128, 128), 256)
    owin = pl.ds(pl.multiple_of((1 - c) * 128, 128), 256)

    def xc_send():
        ref = xbuf.at[:, :, :, c, :, :, owin]
        send(ref, ref, xc_s, xc_r, partner)

    def xc_wait():
        ref = xbuf.at[:, :, :, 1 - c, :, :, win]
        arrived(ref, xc_s, xc_r, partner)

    def t4(p):
        xt[...] = xbuf[kp[p], :, :, :, :, :, win].reshape(512, 256).T

        def step(n, _):
            col = pl.ds(pl.multiple_of(n * 512, 512), 512)
            rhs = gbuf[kp[p], :, :, :, :, col].reshape(512, 512)
            out = jnp.dot(xt[...], rhs, preferred_element_type=F32)
            if p == 0:
                acc[:, col] = out
            else:
                acc[:, col] += out
            return 0

        lax.fori_loop(0, 3, step, 0)

    xa_send(1)
    xa_send(3)
    ring_start(0)
    ye_send(1)
    ye_send(3)
    loads[0].wait()
    loads[1].wait()
    xa_wait(1)
    xa_wait(3)
    xa_send(2)
    ye_send(2)
    ring_adv(0, 1)
    ye_wait(3)
    ring_start(1)
    ring_adv(0, 2)
    xa_wait(2)
    ref = xbuf.at[:, yl, zq, c, zh]
    send(ref, ref, yl_s, yl_r, yldev)
    ring_adv(1, 1)
    arrived(xbuf.at[:, 1 - yl, zq, c, zh], yl_s, yl_r, yldev)
    z_start()
    ring_adv(0, 3)
    ring_adv(1, 2)
    ye_wait(1)
    ring_start(2)
    z_adv(1)
    loads[2].wait()
    ring_adv(0, 4)
    t3_dot(0)
    ring_adv(1, 3)
    ring_adv(2, 1)
    t3_dot(1)
    ye_wait(2)
    ring_start(3)
    z_adv(2)
    ring_adv(1, 4)
    t3_dot(2)
    ring_adv(2, 2)
    t3_send()
    ring_adv(3, 1)
    z_adv(3)
    ring_adv(2, 3)
    z_adv(4)
    xc_send()
    late = None
    for n, d in enumerate(order):
        t3_pair(d)
        if late is not None:
            t3_out(late)
        late = d
        if n == 3:
            ring_adv(3, 2)
    ring_adv(2, 4)
    ring_adv(3, 3)
    xc_wait()
    for p in range(3):
        cc_wait(p)
        t4(p)
    t3_final()
    ring_adv(3, 4)
    cc_wait(3)
    t4(3)
    gw_out[...] = acc[pl.ds(pl.multiple_of(c * 64, 64), 192), :]
    for cp in sends:
        cp.wait_send()


def body(saved_input, grad_out, weight, samples, correct, prompt_ids):
    w = lax.axis_index("width")
    own_ids = lax.dynamic_slice(prompt_ids, (w * 32,), (32,))
    weights_own = token_weights(own_ids, samples, correct)
    scaled = (grad_out.astype(F32) * weights_own[:, None]).astype(BF16).reshape(2, 16, 1536)
    dma = pltpu.SemaphoreType.DMA
    vm = pl.BlockSpec(memory_space=pltpu.VMEM)
    gw, gi = pl.pallas_call(
        kernel,
        out_shape=(
            jax.ShapeDtypeStruct((192, 1536), F32),
            jax.ShapeDtypeStruct((16, 1536), BF16),
        ),
        in_specs=[vm, vm, pl.BlockSpec(memory_space=pl.ANY)],
        out_specs=(vm, vm),
        scratch_shapes=[
            pltpu.VMEM((NK, NX, 2, 2, 16, 1536), BF16),
            pltpu.VMEM((NK, 2, 4, 2, 2, 16, 384), BF16),
            pltpu.VMEM((1536, 1536), BF16),
            pltpu.VMEM((2, NZ, 16, 1536), BF16),
            pltpu.VMEM((NZ, 16, 1536), BF16),
            pltpu.VMEM((NZ, 16, 1536), BF16),
            pltpu.VMEM((NZ, 16, 1536), BF16),
            pltpu.VMEM((256, 1536), F32),
            pltpu.VMEM((256, 512), BF16),
            dma((3,)),
            dma((4, 2, HALF)), dma((4, 2, HALF)),
            dma((4, 1 + 2 * HALF)), dma((4, 1 + 2 * HALF)),
            dma((3,)), dma((3,)),
            dma((3,)), dma((3,)),
            dma, dma,
            dma((2, HALF)), dma((2, HALF)),
            dma, dma,
            dma((NZ,)), dma((NZ,)),
            dma((NZ,)), dma((NZ,)),
        ],
        compiler_params=pltpu.CompilerParams(
            collective_id=0, has_side_effects=True, vmem_limit_bytes=56 * 1024 * 1024
        ),
        cost_estimate=pl.CostEstimate(flops=3_000_000_000, bytes_accessed=8_000_000, transcendentals=0),
    )(scaled, saved_input, weight)
    return gi, gw


def solution(mesh):
    in_specs = (
        P(("replica", "hidden"), "width"),
        P(("replica", "width"), "hidden"),
        P("width", "hidden"),
        P(),
        P(),
        P("replica"),
    )
    out_specs = (P(("replica", "hidden"), "width"), P(("width", "replica"), "hidden"))
    return jax.shard_map(body, mesh=mesh, in_specs=in_specs, out_specs=out_specs, check_vma=False)
```

```python
import jax
import jax.numpy as jnp
from jax import lax
from jax.experimental import pallas as pl
from jax.experimental.pallas import tpu as pltpu
from jax.sharding import PartitionSpec as P

K = 4
MESH = pl.DeviceIdType.MESH
F32 = jnp.float32
BF16 = jnp.bfloat16

NX = 8
NZ = 8
NK = 4
HALF = NX // 2


def kernel(
    g_in, x_in, w_hbm, smp, cor, ids, gw_out, gi_out,
    g_own, gbuf, xbuf, wv, part, rb1, sb, rb2, acc, xt,
    loc_sem, ring_s, ring_r, co_s, co_r, cc_s, cc_r, ye_s, ye_r, xa_s, xa_r,
    yl_s, yl_r, zr_s, zr_r, xc_s, xc_r, t1_s, t1_r, t2_s, t2_r, in_sem,
):
    h = lax.axis_index("hidden")
    w = lax.axis_index("width")
    r = lax.axis_index("replica")
    k, c = r // 2, lax.rem(r, 2)
    yl, z = h // NZ, lax.rem(h, NZ)
    zq, zh = z // 2, lax.rem(z, 2)

    def xdev(d):
        return {"width": lax.rem(w + d + NX, NX)}

    def zdev(d):
        return {"hidden": yl * NZ + lax.rem(z + d, NZ)}

    def kdev(d):
        return {"replica": lax.rem(k + d, NK) * 2 + c}

    partner = {"replica": k * 2 + 1 - c}
    yldev = {"hidden": (1 - yl) * NZ + z}
    sends = []

    def send(src, dst, ss, rs, dev):
        cp = pltpu.make_async_remote_copy(
            src_ref=src, dst_ref=dst, send_sem=ss, recv_sem=rs, device_id=dev, device_id_type=MESH
        )
        cp.start()
        sends.append(cp)

    def arrived(dst, ss, rs, dev):
        pltpu.make_async_remote_copy(
            src_ref=dst, dst_ref=dst, send_sem=ss, recv_sem=rs, device_id=dev, device_id_type=MESH
        ).wait_recv()

    shift = (0, 1, 3, 2)
    kp = [lax.rem(k + s, NK) for s in shift]

    bar = pltpu.get_barrier_semaphore()
    for dev in (xdev(1), xdev(-1), kdev(1), kdev(3), yldev, partner):
        pl.semaphore_signal(bar, inc=1, device_id=dev, device_id_type=MESH)
    for d in range(1, NZ):

        @pl.when(z + d < NZ)
        def _():
            pl.semaphore_signal(bar, inc=1, device_id=zdev(d), device_id_type=MESH)

    loads = [
        pltpu.make_async_copy(
            x_in.at[:, pl.ds(pl.multiple_of(k * 384, 384), 384)], xbuf.at[k, yl, zq, c, zh], loc_sem.at[1]
        ),
        pltpu.make_async_copy(w_hbm, wv, loc_sem.at[2]),
    ]
    for cp in loads:
        cp.start()

    total = smp[...].astype(F32)
    good = cor[...].astype(F32)
    missing = jnp.ones_like(total)
    for j in range(K):
        missing = missing * jnp.maximum(total - good - j, 0.0) / (total - j)
    pass_at_k = 1.0 - missing
    prompts = lax.broadcasted_iota(jnp.int32, (64, 64), 0) == lax.broadcasted_iota(jnp.int32, (64, 64), 1)
    column = jnp.sum(jnp.where(prompts, jnp.broadcast_to(pass_at_k, (64, 64)), 0.0), axis=1, keepdims=True)
    match = lax.broadcasted_iota(jnp.int32, (64, 256), 0) == jnp.broadcast_to(ids[...], (64, 256))
    picked = jnp.sum(jnp.where(match, jnp.broadcast_to(column, (64, 256)), 0.0), axis=0, keepdims=True)
    rows = lax.broadcasted_iota(jnp.int32, (32, 256), 0) + w * 32
    mine = rows == lax.broadcasted_iota(jnp.int32, (32, 256), 1)
    weight = jnp.sum(jnp.where(mine, jnp.broadcast_to(picked, (32, 256)), 0.0), axis=1, keepdims=True)
    weight = weight.astype(BF16).astype(F32)
    g_own[...] = (g_in[...].astype(F32) * weight).astype(BF16).reshape(2, 16, 1536)

    pl.semaphore_wait(bar, 6 + z)
    for d in range(1, NZ):

        @pl.when(z + d >= NZ)
        def _():
            pl.semaphore_signal(in_sem, inc=1, device_id=zdev(d), device_id_type=MESH)

    def xa_send(d):
        to = lax.rem(k + d, NK)
        send(
            x_in.at[:, pl.ds(pl.multiple_of(to * 384, 384), 384)],
            xbuf.at[k, yl, zq, c, zh], xa_s.at[d - 1], xa_r.at[d - 1], kdev(d),
        )

    def xa_wait(d):
        frm = lax.rem(k + NK - d, NK)
        arrived(xbuf.at[frm, yl, zq, c, zh], xa_s.at[d - 1], xa_r.at[d - 1], kdev(d))

    def ye_send(d):
        send(g_own, gbuf.at[k, w, c], ye_s.at[d - 1], ye_r.at[d - 1], kdev(d))

    def ye_wait(d):
        frm = lax.rem(k + NK - d, NK)
        arrived(gbuf.at[frm, w, c], ye_s.at[d - 1], ye_r.at[d - 1], kdev(d))

    def blk(p, e, s, j, cc):
        m = lax.rem(w - e * s + NX, NX)
        return gbuf.at[kp[p], m, cc, j]

    def halves(i, s):
        return (0, 1) if s < HALF else (i,)

    def ring_start(p):
        own = gbuf.at[kp[p], w, c]
        for j in (0, 1):
            for i, e in enumerate((1, -1)):
                src = g_own.at[j] if p == 0 else own.at[j]
                send(src, own.at[j], ring_s.at[p, i, 0, j], ring_r.at[p, i, 0, j], xdev(e))
        send(g_own if p == 0 else own, own, co_s.at[p], co_r.at[p], partner)

    def ring_adv(p, s):
        for j in (0, 1):
            for i, e in enumerate((1, -1)):
                if j not in halves(i, s):
                    continue
                ref = blk(p, e, s, j, c)
                arrived(ref, ring_s.at[p, i, s - 1, j], ring_r.at[p, i, s - 1, j], xdev(e))
                if s < HALF and j in halves(i, s + 1):
                    send(ref, ref, ring_s.at[p, i, s, j], ring_r.at[p, i, s, j], xdev(e))
                send(ref, ref, cc_s.at[p, i, s - 1, j], cc_r.at[p, i, s - 1, j], partner)

    def cc_wait(p):
        arrived(gbuf.at[kp[p], w, 1 - c], co_s.at[p], co_r.at[p], partner)
        for s in range(1, HALF + 1):
            for i, e in enumerate((1, -1)):
                for j in halves(i, s):
                    ref = blk(p, e, s, j, 1 - c)
                    arrived(ref, cc_s.at[p, i, s - 1, j], cc_r.at[p, i, s - 1, j], partner)

    def z_send(above):
        ref = xbuf.at[:, :, zq, c, zh]
        for d in (4, 3, 5, 2, 6, 1, 7):

            @pl.when(z + d < NZ if above else z + d >= NZ)
            def _():
                pltpu.make_async_remote_copy(
                    src_ref=ref, dst_ref=ref, send_sem=zr_s.at[d], recv_sem=zr_r.at[d],
                    device_id=zdev(d), device_id_type=MESH,
                ).start()

    def z_wait():
        for d in range(1, NZ):
            zz = lax.rem(z + NZ - d, NZ)
            arrived(xbuf.at[:, :, zz // 2, c, lax.rem(zz, 2)], zr_s.at[d], zr_r.at[d], zdev(d))

    def z_sent():
        ref = xbuf.at[:, :, zq, c, zh]
        for d in range(1, NZ):
            pltpu.make_async_remote_copy(
                src_ref=ref, dst_ref=ref, send_sem=zr_s.at[d], recv_sem=zr_r.at[d],
                device_id=zdev(d), device_id_type=MESH,
            ).wait_send()

    def t3_dot(n):
        lhs = gbuf[k, :, c].reshape(256, 1536)
        out = lax.dot_general(
            lhs, wv[pl.ds(n * 512, 512), :], (((1,), (1,)), ((), ())), preferred_element_type=F32
        )
        part[:, :, :, pl.ds(n * 512, 512)] = out.astype(BF16).reshape(2, NZ, 16, 512)

    order = (4, 3, 5, 2, 6, 1, 7, 0)

    def t3_send():
        for d in order:
            zz = lax.rem(z + d, NZ)
            send(part.at[1 - yl, zz], rb1.at[d], t1_s.at[d], t1_r.at[d], yldev)

    def t3_pair(d):
        zz = lax.rem(z + d, NZ)
        arrived(rb1.at[d], t1_s.at[d], t1_r.at[d], yldev)
        both = part[yl, zz].astype(F32) + rb1[d].astype(F32)
        sb[d] = both.astype(BF16)

    def t3_out(d):
        if d:
            send(sb.at[d], rb2.at[d], t2_s.at[d], t2_r.at[d], zdev(d))

    def t3_final():
        total = sb[0].astype(F32)
        for d in range(1, NZ):
            arrived(rb2.at[d], t2_s.at[d], t2_r.at[d], zdev(d))
            total = total + rb2[d].astype(F32)
        gi_out[...] = total.astype(BF16)

    win = pl.ds(pl.multiple_of(c * 128, 128), 256)
    owin = pl.ds(pl.multiple_of((1 - c) * 128, 128), 256)

    def xc_send():
        ref = xbuf.at[:, :, :, c, :, :, owin]
        send(ref, ref, xc_s, xc_r, partner)

    def xc_wait():
        ref = xbuf.at[:, :, :, 1 - c, :, :, win]
        arrived(ref, xc_s, xc_r, partner)

    def t4(p):
        xt[...] = xbuf[kp[p], :, :, :, :, :, win].reshape(512, 256).T

        def step(n, _):
            col = pl.ds(pl.multiple_of(n * 512, 512), 512)
            rhs = gbuf[kp[p], :, :, :, :, col].reshape(512, 512)
            out = jnp.dot(xt[...], rhs, preferred_element_type=F32)
            if p == 0:
                acc[:, col] = out
            else:
                acc[:, col] += out
            return 0

        lax.fori_loop(0, 3, step, 0)

    ring_start(0)
    xa_send(1)
    xa_send(3)
    ye_send(1)
    ye_send(3)
    keep = pltpu.make_async_copy(g_own, gbuf.at[k, w, c], loc_sem.at[0])
    keep.start()
    xa_wait(1)
    xa_wait(3)
    xa_send(2)
    ye_send(2)
    ring_adv(0, 1)
    loads[0].wait()
    ring_adv(0, 2)
    xa_wait(2)
    ref = xbuf.at[:, yl, zq, c, zh]
    send(ref, ref, yl_s, yl_r, yldev)
    ring_adv(0, 3)
    arrived(xbuf.at[:, 1 - yl, zq, c, zh], yl_s, yl_r, yldev)
    z_send(False)
    ye_wait(3)
    ring_start(1)
    ye_wait(1)
    ring_start(2)
    loads[1].wait()
    keep.wait()
    ring_adv(0, 4)
    t3_dot(0)
    t3_dot(1)
    ring_adv(1, 1)
    t3_dot(2)
    ring_adv(2, 1)
    t3_send()
    ye_wait(2)
    ring_start(3)

    @pl.when(z < NZ - 1)
    def _():
        pl.semaphore_wait(in_sem, NZ - 1 - z)

    z_send(True)
    ring_adv(1, 2)
    late = None
    for n, d in enumerate(order):
        t3_pair(d)
        if late is not None:
            t3_out(late)
        late = d
        if n == 2:
            ring_adv(2, 2)
        if n == 4:
            ring_adv(3, 1)
        if n == 6:
            ring_adv(1, 3)
    ring_adv(2, 3)
    ring_adv(3, 2)
    ring_adv(1, 4)
    ring_adv(2, 4)
    ring_adv(3, 3)
    ring_adv(3, 4)
    z_wait()
    xc_send()
    xc_wait()
    for p in range(4):
        cc_wait(p)
        t4(p)
    gw_out[...] = acc[pl.ds(pl.multiple_of(c * 64, 64), 192), :]
    t3_final()
    z_sent()
    for cp in sends:
        cp.wait_send()


def body(saved_input, grad_out, weight, samples, correct, prompt_ids):
    dma = pltpu.SemaphoreType.DMA
    vm = pl.BlockSpec(memory_space=pltpu.VMEM)
    gw, gi = pl.pallas_call(
        kernel,
        out_shape=(
            pltpu.VMEM((192, 1536), F32),
            pltpu.VMEM((16, 1536), BF16),
        ),
        in_specs=[vm, vm, pl.BlockSpec(memory_space=pl.ANY), vm, vm, vm],
        out_specs=(vm, vm),
        scratch_shapes=[
            pltpu.VMEM((2, 16, 1536), BF16),
            pltpu.VMEM((NK, NX, 2, 2, 16, 1536), BF16),
            pltpu.VMEM((NK, 2, 4, 2, 2, 16, 384), BF16),
            pltpu.VMEM((1536, 1536), BF16),
            pltpu.VMEM((2, NZ, 16, 1536), BF16),
            pltpu.VMEM((NZ, 16, 1536), BF16),
            pltpu.VMEM((NZ, 16, 1536), BF16),
            pltpu.VMEM((NZ, 16, 1536), BF16),
            pltpu.VMEM((256, 1536), F32),
            pltpu.VMEM((256, 512), BF16),
            dma((3,)),
            dma((4, 2, HALF, 2)), dma((4, 2, HALF, 2)),
            dma((4,)), dma((4,)),
            dma((4, 2, HALF, 2)), dma((4, 2, HALF, 2)),
            dma((3,)), dma((3,)),
            dma((3,)), dma((3,)),
            dma, dma,
            dma((NZ,)), dma((NZ,)),
            dma, dma,
            dma((NZ,)), dma((NZ,)),
            dma((NZ,)), dma((NZ,)),
            pltpu.SemaphoreType.REGULAR,
        ],
        compiler_params=pltpu.CompilerParams(
            collective_id=0, has_side_effects=True, vmem_limit_bytes=56 * 1024 * 1024
        ),
        cost_estimate=pl.CostEstimate(flops=3_000_000_000, bytes_accessed=8_000_000, transcendentals=0),
    )(grad_out, saved_input, weight, samples[None, :], correct[None, :], prompt_ids[None, :])
    return gi, gw


def solution(mesh):
    in_specs = (
        P(("replica", "hidden"), "width"),
        P(("replica", "width"), "hidden"),
        P("width", "hidden"),
        P(),
        P(),
        P("replica"),
    )
    out_specs = (P(("replica", "hidden"), "width"), P(("width", "replica"), "hidden"))
    return jax.shard_map(body, mesh=mesh, in_specs=in_specs, out_specs=out_specs, check_vma=False)
```

```python
import jax
import jax.numpy as jnp
from jax import lax
from jax.experimental import pallas as pl
from jax.experimental.pallas import tpu as pltpu
from jax.sharding import PartitionSpec as P

K = 4
MESH = pl.DeviceIdType.MESH
F32 = jnp.float32
BF16 = jnp.bfloat16

NX = 8
NZ = 8
NK = 4
HALF = NX // 2


def kernel(
    g_in, x_in, w_hbm, smp, cor, ids, gw_out, gi_out,
    g_raw, g_own, gbuf, xbuf, wv, part, rb1, sb, rb2, acc, xt,
    loc_sem, ring_s, ring_r, co_s, co_r, cc_s, cc_r, ye_s, ye_r, xa_s, xa_r, an_s, an_r,
    zr_s, zr_r, xc_s, xc_r, t1_s, t1_r, t2_s, t2_r, in_sem, pin_sem,
):
    h = lax.axis_index("hidden")
    w = lax.axis_index("width")
    r = lax.axis_index("replica")
    k, c = r // 2, lax.rem(r, 2)
    yl, z = h // NZ, lax.rem(h, NZ)
    zq, zh = z // 2, lax.rem(z, 2)

    def xdev(d):
        return {"width": lax.rem(w + d + NX, NX)}

    def zdev(d):
        return {"hidden": yl * NZ + lax.rem(z + d, NZ)}

    def kdev(d):
        return {"replica": lax.rem(k + d, NK) * 2 + c}

    partner = {"replica": k * 2 + 1 - c}
    yldev = {"hidden": (1 - yl) * NZ + z}
    sends = []

    def send(src, dst, ss, rs, dev):
        cp = pltpu.make_async_remote_copy(
            src_ref=src, dst_ref=dst, send_sem=ss, recv_sem=rs, device_id=dev, device_id_type=MESH
        )
        cp.start()
        sends.append(cp)

    def arrived(dst, ss, rs, dev):
        pltpu.make_async_remote_copy(
            src_ref=dst, dst_ref=dst, send_sem=ss, recv_sem=rs, device_id=dev, device_id_type=MESH
        ).wait_recv()

    shift = (0, 1, 3, 2)
    kp = [lax.rem(k + s, NK) for s in shift]

    bar = pltpu.get_barrier_semaphore()
    y_peers = [(dk, dy) for dk in (1, 3, 2, 0) for dy in (0, 1) if dk or dy]

    def ydev(dk, dy):
        return {"hidden": (1 - yl if dy else yl) * NZ + z, **kdev(dk)}

    for dev in (xdev(1), xdev(-1), *(ydev(*at) for at in y_peers)):
        pl.semaphore_signal(bar, inc=1, device_id=dev, device_id_type=MESH)

    @pl.when(c == 1)
    def _():
        pl.semaphore_signal(bar, inc=1, device_id=partner, device_id_type=MESH)

    for d in range(1, NZ):

        @pl.when(z + d < NZ)
        def _():
            pl.semaphore_signal(bar, inc=1, device_id=zdev(d), device_id_type=MESH)

    loads = [
        pltpu.make_async_copy(
            x_in.at[:, pl.ds(pl.multiple_of(k * 384, 384), 384)], xbuf.at[k, yl, zq, c, zh], loc_sem.at[1]
        ),
        pltpu.make_async_copy(w_hbm, wv, loc_sem.at[2]),
    ]
    raw = pltpu.make_async_copy(g_in, g_raw, loc_sem.at[3])
    raw.start()
    for cp in loads:
        cp.start()

    pl.semaphore_wait(bar, 10 - c + z)

    @pl.when(c == 0)
    def _():
        pl.semaphore_signal(pin_sem, inc=1, device_id=partner, device_id_type=MESH)

    for d in range(1, NZ):

        @pl.when(z + d >= NZ)
        def _():
            pl.semaphore_signal(in_sem, inc=1, device_id=zdev(d), device_id_type=MESH)

    def xa_copy(n, dk, dy):
        to = lax.rem(k + dk, NK)
        return pltpu.make_async_remote_copy(
            src_ref=x_in.at[:, pl.ds(pl.multiple_of(to * 384, 384), 384)],
            dst_ref=xbuf.at[k, yl, zq, c, zh],
            send_sem=xa_s.at[n], recv_sem=xa_r.at[n], device_id=ydev(dk, dy), device_id_type=MESH,
        )

    def xa_wait():
        for n, (dk, dy) in enumerate(y_peers):
            frm = lax.rem(k + NK - dk, NK)
            arrived(xbuf.at[frm, 1 - yl if dy else yl, zq, c, zh], xa_s.at[n], xa_r.at[n], partner)

    for n, at in enumerate(y_peers):
        cp = xa_copy(n, *at)
        cp.start()
        sends.append(cp)

    total = smp[...].astype(F32)
    good = cor[...].astype(F32)
    missing = jnp.ones_like(total)
    for j in range(K):
        missing = missing * jnp.maximum(total - good - j, 0.0) / (total - j)
    pass_at_k = 1.0 - missing
    prompts = lax.broadcasted_iota(jnp.int32, (64, 64), 0) == lax.broadcasted_iota(jnp.int32, (64, 64), 1)
    column = jnp.sum(jnp.where(prompts, jnp.broadcast_to(pass_at_k, (64, 64)), 0.0), axis=1, keepdims=True)
    match = lax.broadcasted_iota(jnp.int32, (64, 256), 0) == jnp.broadcast_to(ids[...], (64, 256))
    picked = jnp.sum(jnp.where(match, jnp.broadcast_to(column, (64, 256)), 0.0), axis=0, keepdims=True)
    rows = lax.broadcasted_iota(jnp.int32, (32, 256), 0) + w * 32
    mine = rows == lax.broadcasted_iota(jnp.int32, (32, 256), 1)
    weight = jnp.sum(jnp.where(mine, jnp.broadcast_to(picked, (32, 256)), 0.0), axis=1, keepdims=True)
    weight = weight.astype(BF16).astype(F32)
    raw.wait()
    g_own[...] = (g_raw[...].astype(F32) * weight).astype(BF16).reshape(2, 16, 1536)

    def ye_send(d):
        send(g_own, gbuf.at[k, w, c], ye_s.at[d - 1], ye_r.at[d - 1], kdev(d))

    def ye_wait(d):
        frm = lax.rem(k + NK - d, NK)
        arrived(gbuf.at[frm, w, c], ye_s.at[d - 1], ye_r.at[d - 1], kdev(d))

    def away(e, s):
        return lax.rem(w - e * s + NX, NX)

    def pieces(p, e, s, cc):
        ref = gbuf.at[kp[p], away(e, s), cc]
        if p in (1, 2):
            return [(0, ref)] if s < HALF else []
        if s < HALF:
            return [(0, ref.at[0]), (1, ref.at[1])]
        j = 0 if e == 1 else 1
        return [(j, ref.at[j])]

    def ring_start(p):
        own = gbuf.at[kp[p], w, c]
        for j in (0,) if p in (1, 2) else (0, 1):
            for i, e in enumerate((1, -1)):
                dst = own if p in (1, 2) else own.at[j]
                src = g_own.at[j] if p == 0 else dst
                send(src, dst, ring_s.at[p, i, 0, j], ring_r.at[p, i, 0, j], xdev(e))

    def ring_adv(p, s):
        for n in (0, 1):
            for i, e in enumerate((1, -1)):
                here = pieces(p, e, s, c)
                if n >= len(here):
                    continue
                j, ref = here[n]
                arrived(ref, ring_s.at[p, i, s - 1, j], ring_r.at[p, i, s - 1, j], xdev(e))
                if s < HALF and j in [q for q, _ in pieces(p, e, s + 1, c)]:
                    send(ref, ref, ring_s.at[p, i, s, j], ring_r.at[p, i, s, j], xdev(e))

    def anti_send():
        ref = gbuf.at[k, away(1, HALF), c]
        for n, d in enumerate((1, 3)):
            send(ref, ref, an_s.at[n], an_r.at[n], kdev(d))

    def anti_wait(p):
        n = 1 if p == 1 else 0
        arrived(gbuf.at[kp[p], away(1, HALF), c], an_s.at[n], an_r.at[n], partner)

    def cc_send(p):
        ref = gbuf.at[kp[p], :, c]
        send(ref, ref, co_s.at[p], co_r.at[p], partner)

    def cc_last(n, e, s):
        ref = gbuf.at[kp[3], away(e, s), c]
        send(ref, ref, cc_s.at[n], cc_r.at[n], partner)

    def cc_wait(p):
        if p < 3:
            arrived(gbuf.at[kp[p], :, 1 - c], co_s.at[p], co_r.at[p], partner)
            return
        for n in range(NX):
            e, s = (1, n) if n <= HALF else (-1, n - HALF)
            arrived(gbuf.at[kp[3], away(e, s), 1 - c], cc_s.at[n], cc_r.at[n], partner)

    def z_send(above):
        ref = xbuf.at[:, :, zq, c, zh]
        for d in (4, 3, 5, 2, 6, 1, 7):

            @pl.when(z + d < NZ if above else z + d >= NZ)
            def _():
                pltpu.make_async_remote_copy(
                    src_ref=ref, dst_ref=ref, send_sem=zr_s.at[d], recv_sem=zr_r.at[d],
                    device_id=zdev(d), device_id_type=MESH,
                ).start()

    def z_wait():
        for d in range(1, NZ):
            zz = lax.rem(z + NZ - d, NZ)
            arrived(xbuf.at[:, :, zz // 2, c, lax.rem(zz, 2)], zr_s.at[d], zr_r.at[d], zdev(d))

    def z_sent():
        ref = xbuf.at[:, :, zq, c, zh]
        for d in range(1, NZ):
            pltpu.make_async_remote_copy(
                src_ref=ref, dst_ref=ref, send_sem=zr_s.at[d], recv_sem=zr_r.at[d],
                device_id=zdev(d), device_id_type=MESH,
            ).wait_send()

    def t3_dot(n):
        lhs = gbuf[k, :, c].reshape(256, 1536)
        out = lax.dot_general(
            lhs, wv[pl.ds(n * 512, 512), :], (((1,), (1,)), ((), ())), preferred_element_type=F32
        )
        part[:, :, :, pl.ds(n * 512, 512)] = out.astype(BF16).reshape(2, NZ, 16, 512)

    order = (4, 3, 5, 2, 6, 1, 7, 0)

    def t3_send():
        for d in order:
            zz = lax.rem(z + d, NZ)
            send(part.at[1 - yl, zz], rb1.at[d], t1_s.at[d], t1_r.at[d], yldev)

    def t3_pair(d):
        zz = lax.rem(z + d, NZ)
        arrived(rb1.at[d], t1_s.at[d], t1_r.at[d], yldev)
        both = part[yl, zz].astype(F32) + rb1[d].astype(F32)
        sb[d] = both.astype(BF16)

    def t3_out(d):
        if d:
            send(sb.at[d], rb2.at[d], t2_s.at[d], t2_r.at[d], zdev(d))

    def t3_final():
        total = sb[0].astype(F32)
        for d in range(1, NZ):
            arrived(rb2.at[d], t2_s.at[d], t2_r.at[d], zdev(d))
            total = total + rb2[d].astype(F32)
        gi_out[...] = total.astype(BF16)

    win = pl.ds(pl.multiple_of(c * 128, 128), 256)
    owin = pl.ds(pl.multiple_of((1 - c) * 128, 128), 256)

    def xc_send():
        ref = xbuf.at[:, :, :, c, :, :, owin]
        send(ref, ref, xc_s, xc_r, partner)

    def xc_wait():
        ref = xbuf.at[:, :, :, 1 - c, :, :, win]
        arrived(ref, xc_s, xc_r, partner)

    def t4(p):
        xt[...] = xbuf[kp[p], :, :, :, :, :, win].reshape(512, 256).T

        def step(n, _):
            col = pl.ds(pl.multiple_of(n * 512, 512), 512)
            rhs = gbuf[kp[p], :, :, :, :, col].reshape(512, 512)
            out = jnp.dot(xt[...], rhs, preferred_element_type=F32)
            if p == 0:
                acc[:, col] = out
            elif p < 3:
                acc[:, col] += out
            else:

                @pl.when(c == 0)
                def _():
                    gw_out[:, col] = acc[pl.ds(0, 192), col] + out[:192]

                @pl.when(c == 1)
                def _():
                    gw_out[:, col] = acc[pl.ds(64, 192), col] + out[64:]

            return 0

        lax.fori_loop(0, 3, step, 0)

    late = []

    def t3_next(count):
        for _ in range(count):
            d = order[len(late)]
            t3_pair(d)
            if late:
                t3_out(late[-1])
            late.append(d)

    ring_start(0)
    ye_send(1)
    ye_send(3)
    ye_send(2)
    keep = pltpu.make_async_copy(g_own, gbuf.at[k, w, c], loc_sem.at[0])
    keep.start()
    ring_adv(0, 1)
    loads[0].wait()
    xa_wait()
    z_send(False)
    ring_adv(0, 2)
    ye_wait(3)
    ring_start(1)
    ring_adv(0, 3)
    ye_wait(1)
    ring_start(2)
    keep.wait()
    loads[1].wait()
    ring_adv(0, 4)
    t3_dot(0)
    t3_dot(1)
    t3_dot(2)
    ring_adv(1, 1)
    t3_send()
    ye_wait(2)
    ring_start(3)
    ring_adv(2, 1)

    @pl.when(z < NZ - 1)
    def _():
        pl.semaphore_wait(in_sem, NZ - 1 - z)

    z_send(True)
    t3_next(2)
    ring_adv(1, 2)
    anti_send()
    t3_next(2)
    ring_adv(3, 1)
    t3_next(2)
    ring_adv(2, 2)
    t3_next(2)
    ring_adv(3, 2)

    @pl.when(c == 1)
    def _():
        pl.semaphore_wait(pin_sem, 1)

    cc_send(0)
    cc_last(0, 1, 0)
    cc_last(1, 1, 1)
    cc_last(5, -1, 1)
    cc_last(2, 1, 2)
    cc_last(6, -1, 2)
    ring_adv(1, 3)
    anti_wait(1)
    cc_send(1)
    ring_adv(2, 3)
    anti_wait(2)
    cc_send(2)
    ring_adv(3, 3)
    cc_last(3, 1, 3)
    cc_last(7, -1, 3)
    z_wait()
    xc_send()
    ring_adv(3, 4)
    cc_last(4, 1, 4)
    xc_wait()
    for p in range(4):
        cc_wait(p)
        t4(p)
    t3_final()
    z_sent()
    for cp in sends:
        cp.wait_send()


def body(saved_input, grad_out, weight, samples, correct, prompt_ids):
    dma = pltpu.SemaphoreType.DMA
    vm = pl.BlockSpec(memory_space=pltpu.VMEM)
    hbm = pl.BlockSpec(memory_space=pl.ANY)
    gw, gi = pl.pallas_call(
        kernel,
        out_shape=(
            pltpu.VMEM((192, 1536), F32),
            pltpu.VMEM((16, 1536), BF16),
        ),
        in_specs=[hbm, hbm, hbm, vm, vm, vm],
        out_specs=(vm, vm),
        scratch_shapes=[
            pltpu.VMEM((32, 1536), BF16),
            pltpu.VMEM((2, 16, 1536), BF16),
            pltpu.VMEM((NK, NX, 2, 2, 16, 1536), BF16),
            pltpu.VMEM((NK, 2, 4, 2, 2, 16, 384), BF16),
            pltpu.VMEM((1536, 1536), BF16),
            pltpu.VMEM((2, NZ, 16, 1536), BF16),
            pltpu.VMEM((NZ, 16, 1536), BF16),
            pltpu.VMEM((NZ, 16, 1536), BF16),
            pltpu.VMEM((NZ, 16, 1536), BF16),
            pltpu.VMEM((256, 1536), F32),
            pltpu.VMEM((256, 512), BF16),
            dma((4,)),
            dma((4, 2, HALF, 2)), dma((4, 2, HALF, 2)),
            dma((3,)), dma((3,)),
            dma((NX,)), dma((NX,)),
            dma((3,)), dma((3,)),
            dma((7,)), dma((7,)),
            dma((2,)), dma((2,)),
            dma((NZ,)), dma((NZ,)),
            dma, dma,
            dma((NZ,)), dma((NZ,)),
            dma((NZ,)), dma((NZ,)),
            pltpu.SemaphoreType.REGULAR,
            pltpu.SemaphoreType.REGULAR,
        ],
        compiler_params=pltpu.CompilerParams(
            collective_id=0, has_side_effects=True, vmem_limit_bytes=56 * 1024 * 1024
        ),
        cost_estimate=pl.CostEstimate(flops=3_000_000_000, bytes_accessed=8_000_000, transcendentals=0),
    )(grad_out, saved_input, weight, samples[None, :], correct[None, :], prompt_ids[None, :])
    return gi, gw


def solution(mesh):
    in_specs = (
        P(("replica", "hidden"), "width"),
        P(("replica", "width"), "hidden"),
        P("width", "hidden"),
        P(),
        P(),
        P("replica"),
    )
    out_specs = (P(("replica", "hidden"), "width"), P(("width", "replica"), "hidden"))
    return jax.shard_map(body, mesh=mesh, in_specs=in_specs, out_specs=out_specs, check_vma=False)
```

```python
import jax
import jax.numpy as jnp
from jax import lax
from jax.experimental import pallas as pl
from jax.experimental.pallas import tpu as pltpu
from jax.sharding import PartitionSpec as P

K = 4
MESH = pl.DeviceIdType.MESH
F32 = jnp.float32
BF16 = jnp.bfloat16

NX = 8
NZ = 8
NK = 4
HALF = NX // 2


def kernel(
    g_in, x_in, w_hbm, smp, cor, ids, gw_out, gi_out,
    v_smp, v_cor, v_ids, g_raw, g_own, gbuf, xbuf, wv, part, rb1, sb, rb2, acc, xt,
    loc_sem, ring_s, ring_r, co_s, co_r, cc_s, cc_r, ye_s, ye_r, xa_s, xa_r, an_s, an_r,
    zr_s, zr_r, xc_s, xc_r, t1_s, t1_r, t2_s, t2_r, in_sem, pin_sem,
):
    h = lax.axis_index("hidden")
    w = lax.axis_index("width")
    r = lax.axis_index("replica")
    k, c = r // 2, lax.rem(r, 2)
    yl, z = h // NZ, lax.rem(h, NZ)
    zq, zh = z // 2, lax.rem(z, 2)

    def xdev(d):
        return {"width": lax.rem(w + d + NX, NX)}

    def zdev(d):
        return {"hidden": yl * NZ + lax.rem(z + d, NZ)}

    def kdev(d):
        return {"replica": lax.rem(k + d, NK) * 2 + c}

    partner = {"replica": k * 2 + 1 - c}
    yldev = {"hidden": (1 - yl) * NZ + z}
    sends = []

    def send(src, dst, ss, rs, dev):
        cp = pltpu.make_async_remote_copy(
            src_ref=src, dst_ref=dst, send_sem=ss, recv_sem=rs, device_id=dev, device_id_type=MESH
        )
        cp.start()
        sends.append(cp)

    def arrived(dst, ss, rs, dev):
        pltpu.make_async_remote_copy(
            src_ref=dst, dst_ref=dst, send_sem=ss, recv_sem=rs, device_id=dev, device_id_type=MESH
        ).wait_recv()

    shift = (0, 1, 3, 2)
    kp = [lax.rem(k + s, NK) for s in shift]

    bar = pltpu.get_barrier_semaphore()
    y_peers = [(dk, dy) for dk in (1, 3, 2, 0) for dy in (0, 1) if dk or dy]

    def ydev(dk, dy):
        return {"hidden": (1 - yl if dy else yl) * NZ + z, **kdev(dk)}

    for dev in (xdev(1), xdev(-1), *(ydev(*at) for at in y_peers)):
        pl.semaphore_signal(bar, inc=1, device_id=dev, device_id_type=MESH)

    @pl.when(c == 1)
    def _():
        pl.semaphore_signal(bar, inc=1, device_id=partner, device_id_type=MESH)

    for d in range(1, NZ):

        @pl.when(z + d < NZ)
        def _():
            pl.semaphore_signal(bar, inc=1, device_id=zdev(d), device_id_type=MESH)

    loads = [
        pltpu.make_async_copy(
            x_in.at[:, pl.ds(pl.multiple_of(k * 384, 384), 384)], xbuf.at[k, yl, zq, c, zh], loc_sem.at[1]
        ),
        pltpu.make_async_copy(w_hbm, wv, loc_sem.at[2]),
    ]
    raw = [
        pltpu.make_async_copy(src, dst, loc_sem.at[3 + n])
        for n, (src, dst) in enumerate(((smp, v_smp), (cor, v_cor), (ids, v_ids), (g_in, g_raw)))
    ]
    for cp in raw:
        cp.start()
    for cp in loads:
        cp.start()

    for cp in raw[:3]:
        cp.wait()
    total = v_smp[...].astype(F32)
    good = v_cor[...].astype(F32)
    missing = jnp.ones_like(total)
    for j in range(K):
        missing = missing * jnp.maximum(total - good - j, 0.0) / (total - j)
    pass_at_k = 1.0 - missing
    prompts = lax.broadcasted_iota(jnp.int32, (64, 64), 0) == lax.broadcasted_iota(jnp.int32, (64, 64), 1)
    column = jnp.sum(jnp.where(prompts, jnp.broadcast_to(pass_at_k, (64, 64)), 0.0), axis=1, keepdims=True)
    match = lax.broadcasted_iota(jnp.int32, (64, 256), 0) == jnp.broadcast_to(v_ids[...], (64, 256))
    picked = jnp.sum(jnp.where(match, jnp.broadcast_to(column, (64, 256)), 0.0), axis=0, keepdims=True)
    rows = lax.broadcasted_iota(jnp.int32, (32, 256), 0) + w * 32
    mine = rows == lax.broadcasted_iota(jnp.int32, (32, 256), 1)
    weight = jnp.sum(jnp.where(mine, jnp.broadcast_to(picked, (32, 256)), 0.0), axis=1, keepdims=True)
    weight = weight.astype(BF16).astype(F32)
    raw[3].wait()
    g_own[...] = (g_raw[...].astype(F32) * weight).astype(BF16).reshape(2, 16, 1536)

    pl.semaphore_wait(bar, 10 - c + z)

    @pl.when(c == 0)
    def _():
        pl.semaphore_signal(pin_sem, inc=1, device_id=partner, device_id_type=MESH)

    for d in range(1, NZ):

        @pl.when(z + d >= NZ)
        def _():
            pl.semaphore_signal(in_sem, inc=1, device_id=zdev(d), device_id_type=MESH)

    def xa_copy(n, dk, dy):
        to = lax.rem(k + dk, NK)
        return pltpu.make_async_remote_copy(
            src_ref=x_in.at[:, pl.ds(pl.multiple_of(to * 384, 384), 384)],
            dst_ref=xbuf.at[k, yl, zq, c, zh],
            send_sem=xa_s.at[n], recv_sem=xa_r.at[n], device_id=ydev(dk, dy), device_id_type=MESH,
        )

    def xa_wait():
        for n, (dk, dy) in enumerate(y_peers):
            frm = lax.rem(k + NK - dk, NK)
            arrived(xbuf.at[frm, 1 - yl if dy else yl, zq, c, zh], xa_s.at[n], xa_r.at[n], partner)

    def ye_send(d):
        send(g_own, gbuf.at[k, w, c], ye_s.at[d - 1], ye_r.at[d - 1], kdev(d))

    def ye_wait(d):
        frm = lax.rem(k + NK - d, NK)
        arrived(gbuf.at[frm, w, c], ye_s.at[d - 1], ye_r.at[d - 1], kdev(d))

    def away(e, s):
        return lax.rem(w - e * s + NX, NX)

    def pieces(p, e, s, cc):
        ref = gbuf.at[kp[p], away(e, s), cc]
        if p in (1, 2):
            return [(0, ref)] if s < HALF else []
        if s < HALF:
            return [(0, ref.at[0]), (1, ref.at[1])]
        j = 0 if e == 1 else 1
        return [(j, ref.at[j])]

    def ring_start(p):
        own = gbuf.at[kp[p], w, c]
        for j in (0,) if p in (1, 2) else (0, 1):
            for i, e in enumerate((1, -1)):
                dst = own if p in (1, 2) else own.at[j]
                src = g_own.at[j] if p == 0 else dst
                send(src, dst, ring_s.at[p, i, 0, j], ring_r.at[p, i, 0, j], xdev(e))

    def ring_adv(p, s):
        for n in (0, 1):
            for i, e in enumerate((1, -1)):
                here = pieces(p, e, s, c)
                if n >= len(here):
                    continue
                j, ref = here[n]
                arrived(ref, ring_s.at[p, i, s - 1, j], ring_r.at[p, i, s - 1, j], xdev(e))
                if s < HALF and j in [q for q, _ in pieces(p, e, s + 1, c)]:
                    send(ref, ref, ring_s.at[p, i, s, j], ring_r.at[p, i, s, j], xdev(e))

    def anti_send():
        ref = gbuf.at[k, away(1, HALF), c]
        for n, d in enumerate((1, 3)):
            send(ref, ref, an_s.at[n], an_r.at[n], kdev(d))

    def anti_wait(p):
        n = 1 if p == 1 else 0
        arrived(gbuf.at[kp[p], away(1, HALF), c], an_s.at[n], an_r.at[n], partner)

    def cc_send(p):
        ref = gbuf.at[kp[p], :, c]
        send(ref, ref, co_s.at[p], co_r.at[p], partner)

    def cc_last(n, e, s):
        ref = gbuf.at[kp[3], away(e, s), c]
        send(ref, ref, cc_s.at[n], cc_r.at[n], partner)

    def cc_wait(p):
        if p < 3:
            arrived(gbuf.at[kp[p], :, 1 - c], co_s.at[p], co_r.at[p], partner)
            return
        for n in range(NX):
            e, s = (1, n) if n <= HALF else (-1, n - HALF)
            arrived(gbuf.at[kp[3], away(e, s), 1 - c], cc_s.at[n], cc_r.at[n], partner)

    def z_send(above):
        ref = xbuf.at[:, :, zq, c, zh]
        for d in (1, 2, 7, 3, 6, 4, 5):

            @pl.when(z + d < NZ if above else z + d >= NZ)
            def _():
                pltpu.make_async_remote_copy(
                    src_ref=ref, dst_ref=ref, send_sem=zr_s.at[d], recv_sem=zr_r.at[d],
                    device_id=zdev(d), device_id_type=MESH,
                ).start()

    def z_wait():
        for d in range(1, NZ):
            zz = lax.rem(z + NZ - d, NZ)
            arrived(xbuf.at[:, :, zz // 2, c, lax.rem(zz, 2)], zr_s.at[d], zr_r.at[d], zdev(d))

    def z_sent():
        ref = xbuf.at[:, :, zq, c, zh]
        for d in range(1, NZ):
            pltpu.make_async_remote_copy(
                src_ref=ref, dst_ref=ref, send_sem=zr_s.at[d], recv_sem=zr_r.at[d],
                device_id=zdev(d), device_id_type=MESH,
            ).wait_send()

    def t3_dot(n):
        lhs = gbuf[k, :, c].reshape(256, 1536)
        out = lax.dot_general(
            lhs, wv[pl.ds(n * 512, 512), :], (((1,), (1,)), ((), ())), preferred_element_type=F32
        )
        part[:, :, :, pl.ds(n * 512, 512)] = out.astype(BF16).reshape(2, NZ, 16, 512)

    order = (1, 2, 7, 3, 6, 4, 5, 0)

    def t3_send():
        for d in order:
            zz = lax.rem(z + d, NZ)
            send(part.at[1 - yl, zz], rb1.at[d], t1_s.at[d], t1_r.at[d], yldev)

    def t3_pair(d):
        zz = lax.rem(z + d, NZ)
        arrived(rb1.at[d], t1_s.at[d], t1_r.at[d], yldev)
        both = part[yl, zz].astype(F32) + rb1[d].astype(F32)
        sb[d] = both.astype(BF16)

    def t3_out(d):
        if d:
            send(sb.at[d], rb2.at[d], t2_s.at[d], t2_r.at[d], zdev(d))

    def t3_final():
        total = sb[0].astype(F32)
        for d in range(1, NZ):
            arrived(rb2.at[d], t2_s.at[d], t2_r.at[d], zdev(d))
            total = total + rb2[d].astype(F32)
        gi_out[...] = total.astype(BF16)

    win = pl.ds(pl.multiple_of(c * 128, 128), 256)
    owin = pl.ds(pl.multiple_of((1 - c) * 128, 128), 256)

    def xc_send():
        ref = xbuf.at[:, :, :, c, :, :, owin]
        send(ref, ref, xc_s, xc_r, partner)

    def xc_wait():
        ref = xbuf.at[:, :, :, 1 - c, :, :, win]
        arrived(ref, xc_s, xc_r, partner)

    def t4(p):
        xt[...] = xbuf[kp[p], :, :, :, :, :, win].reshape(512, 256).T

        def step(n, _):
            col = pl.ds(pl.multiple_of(n * 512, 512), 512)
            rhs = gbuf[kp[p], :, :, :, :, col].reshape(512, 512)
            out = jnp.dot(xt[...], rhs, preferred_element_type=F32)
            if p == 0:
                acc[:, col] = out
            elif p < 3:
                acc[:, col] += out
            else:

                @pl.when(c == 0)
                def _():
                    gw_out[:, col] = acc[pl.ds(0, 192), col] + out[:192]

                @pl.when(c == 1)
                def _():
                    gw_out[:, col] = acc[pl.ds(64, 192), col] + out[64:]

            return 0

        lax.fori_loop(0, 3, step, 0)

    late = []

    def t3_next(count):
        for _ in range(count):
            d = order[len(late)]
            t3_pair(d)
            if late:
                t3_out(late[-1])
            late.append(d)

    ring_start(0)
    for n, at in enumerate(y_peers):
        cp = xa_copy(n, *at)
        cp.start()
        sends.append(cp)
    ye_send(1)
    ye_send(3)
    ye_send(2)
    keep = pltpu.make_async_copy(g_own, gbuf.at[k, w, c], loc_sem.at[0])
    keep.start()
    ring_adv(0, 1)
    loads[0].wait()
    xa_wait()
    z_send(False)
    ring_adv(0, 2)
    ring_adv(0, 3)
    ye_wait(3)
    ring_start(1)
    ye_wait(1)
    ring_start(2)
    ring_adv(0, 4)
    ye_wait(2)
    ring_start(3)
    keep.wait()
    loads[1].wait()
    t3_dot(0)
    t3_dot(1)
    t3_dot(2)
    t3_send()
    anti_send()
    ring_adv(1, 1)
    ring_adv(2, 1)

    @pl.when(z < NZ - 1)
    def _():
        pl.semaphore_wait(in_sem, NZ - 1 - z)

    z_send(True)
    t3_next(2)
    ring_adv(1, 2)
    t3_next(1)
    ring_adv(3, 1)
    t3_next(2)
    ring_adv(2, 2)
    t3_next(2)
    ring_adv(3, 2)

    @pl.when(c == 1)
    def _():
        pl.semaphore_wait(pin_sem, 1)

    cc_send(0)
    cc_last(0, 1, 0)
    cc_last(1, 1, 1)
    cc_last(5, -1, 1)
    cc_last(2, 1, 2)
    cc_last(6, -1, 2)
    t3_next(1)
    ring_adv(1, 3)
    anti_wait(1)
    cc_send(1)
    ring_adv(2, 3)
    ring_adv(3, 3)
    z_wait()
    xc_send()
    anti_wait(2)
    cc_send(2)
    cc_last(3, 1, 3)
    cc_last(7, -1, 3)
    xc_wait()
    cc_wait(0)
    t4(0)
    cc_wait(1)
    t4(1)
    ring_adv(3, 4)
    cc_last(4, 1, 4)
    cc_wait(2)
    t4(2)
    cc_wait(3)
    t4(3)
    t3_final()
    z_sent()
    for cp in sends:
        cp.wait_send()


def body(saved_input, grad_out, weight, samples, correct, prompt_ids):
    dma = pltpu.SemaphoreType.DMA
    vm = pl.BlockSpec(memory_space=pltpu.VMEM)
    hbm = pl.BlockSpec(memory_space=pl.ANY)
    gw, gi = pl.pallas_call(
        kernel,
        out_shape=(
            pltpu.VMEM((192, 1536), F32),
            pltpu.VMEM((16, 1536), BF16),
        ),
        in_specs=[hbm] * 6,
        out_specs=(vm, vm),
        scratch_shapes=[
            pltpu.VMEM((1, 64), jnp.int32),
            pltpu.VMEM((1, 64), jnp.int32),
            pltpu.VMEM((1, 256), jnp.int32),
            pltpu.VMEM((32, 1536), BF16),
            pltpu.VMEM((2, 16, 1536), BF16),
            pltpu.VMEM((NK, NX, 2, 2, 16, 1536), BF16),
            pltpu.VMEM((NK, 2, 4, 2, 2, 16, 384), BF16),
            pltpu.VMEM((1536, 1536), BF16),
            pltpu.VMEM((2, NZ, 16, 1536), BF16),
            pltpu.VMEM((NZ, 16, 1536), BF16),
            pltpu.VMEM((NZ, 16, 1536), BF16),
            pltpu.VMEM((NZ, 16, 1536), BF16),
            pltpu.VMEM((256, 1536), F32),
            pltpu.VMEM((256, 512), BF16),
            dma((7,)),
            dma((4, 2, HALF, 2)), dma((4, 2, HALF, 2)),
            dma((3,)), dma((3,)),
            dma((NX,)), dma((NX,)),
            dma((3,)), dma((3,)),
            dma((7,)), dma((7,)),
            dma((2,)), dma((2,)),
            dma((NZ,)), dma((NZ,)),
            dma, dma,
            dma((NZ,)), dma((NZ,)),
            dma((NZ,)), dma((NZ,)),
            pltpu.SemaphoreType.REGULAR,
            pltpu.SemaphoreType.REGULAR,
        ],
        compiler_params=pltpu.CompilerParams(
            collective_id=0, has_side_effects=True, vmem_limit_bytes=56 * 1024 * 1024
        ),
        cost_estimate=pl.CostEstimate(flops=3_000_000_000, bytes_accessed=8_000_000, transcendentals=0),
    )(grad_out, saved_input, weight, samples[None, :], correct[None, :], prompt_ids[None, :])
    return gi, gw


def solution(mesh):
    in_specs = (
        P(("replica", "hidden"), "width"),
        P(("replica", "width"), "hidden"),
        P("width", "hidden"),
        P(),
        P(),
        P("replica"),
    )
    out_specs = (P(("replica", "hidden"), "width"), P(("width", "replica"), "hidden"))
    return jax.shard_map(body, mesh=mesh, in_specs=in_specs, out_specs=out_specs, check_vma=False)
```

```python
import jax
import jax.numpy as jnp
from jax import lax
from jax.experimental import pallas as pl
from jax.experimental.pallas import tpu as pltpu
from jax.sharding import PartitionSpec as P

K = 4
MESH = pl.DeviceIdType.MESH
F32 = jnp.float32
BF16 = jnp.bfloat16

NX = 8
NZ = 8
NK = 4
HALF = NX // 2


def kernel(
    g_in, x_in, w_hbm, smp, cor, ids, gw_out, gi_out,
    v_smp, v_cor, v_ids, g_raw, g_own, gbuf, xbuf, wv, part, rb1, sb, rb2, acc, xt,
    loc_sem, ring_s, ring_r, co_s, co_r, cc_s, cc_r, ye_s, ye_r, xa_s, xa_r, an_s, an_r,
    zr_s, zr_r, xc_s, xc_r, t1_s, t1_r, t2_s, t2_r, in_sem, pin_sem,
):
    h = lax.axis_index("hidden")
    w = lax.axis_index("width")
    r = lax.axis_index("replica")
    k, c = r // 2, lax.rem(r, 2)
    yl, z = h // NZ, lax.rem(h, NZ)
    zq, zh = z // 2, lax.rem(z, 2)

    def xdev(d):
        return {"width": lax.rem(w + d + NX, NX)}

    def zdev(d):
        return {"hidden": yl * NZ + lax.rem(z + d, NZ)}

    def kdev(d):
        return {"replica": lax.rem(k + d, NK) * 2 + c}

    partner = {"replica": k * 2 + 1 - c}
    yldev = {"hidden": (1 - yl) * NZ + z}
    sends = []

    def send(src, dst, ss, rs, dev):
        cp = pltpu.make_async_remote_copy(
            src_ref=src, dst_ref=dst, send_sem=ss, recv_sem=rs, device_id=dev, device_id_type=MESH
        )
        cp.start()
        sends.append(cp)

    def arrived(dst, ss, rs, dev):
        pltpu.make_async_remote_copy(
            src_ref=dst, dst_ref=dst, send_sem=ss, recv_sem=rs, device_id=dev, device_id_type=MESH
        ).wait_recv()

    shift = (0, 1, 3, 2)
    kp = [lax.rem(k + s, NK) for s in shift]

    bar = pltpu.get_barrier_semaphore()
    y_peers = [(dk, dy) for dk in (1, 3, 2, 0) for dy in (0, 1) if dk or dy]

    def ydev(dk, dy):
        return {"hidden": (1 - yl if dy else yl) * NZ + z, **kdev(dk)}

    for dev in (xdev(1), xdev(-1), *(ydev(*at) for at in y_peers)):
        pl.semaphore_signal(bar, inc=1, device_id=dev, device_id_type=MESH)

    @pl.when(c == 1)
    def _():
        pl.semaphore_signal(bar, inc=1, device_id=partner, device_id_type=MESH)

    for d in range(1, NZ):

        @pl.when(z + d < NZ)
        def _():
            pl.semaphore_signal(bar, inc=1, device_id=zdev(d), device_id_type=MESH)

    loads = [
        pltpu.make_async_copy(
            x_in.at[:, pl.ds(pl.multiple_of(k * 384, 384), 384)], xbuf.at[k, yl, zq, c, zh], loc_sem.at[1]
        ),
        pltpu.make_async_copy(w_hbm, wv, loc_sem.at[2]),
    ]
    raw = [
        pltpu.make_async_copy(src, dst, loc_sem.at[3 + n])
        for n, (src, dst) in enumerate(((smp, v_smp), (cor, v_cor), (ids, v_ids), (g_in, g_raw)))
    ]
    for cp in raw:
        cp.start()
    for cp in loads:
        cp.start()

    for cp in raw[:3]:
        cp.wait()
    total = v_smp[...].astype(F32)
    good = v_cor[...].astype(F32)
    missing = jnp.ones_like(total)
    for j in range(K):
        missing = missing * jnp.maximum(total - good - j, 0.0) / (total - j)
    pass_at_k = 1.0 - missing
    prompts = lax.broadcasted_iota(jnp.int32, (64, 64), 0) == lax.broadcasted_iota(jnp.int32, (64, 64), 1)
    column = jnp.sum(jnp.where(prompts, jnp.broadcast_to(pass_at_k, (64, 64)), 0.0), axis=1, keepdims=True)
    match = lax.broadcasted_iota(jnp.int32, (64, 256), 0) == jnp.broadcast_to(v_ids[...], (64, 256))
    picked = jnp.sum(jnp.where(match, jnp.broadcast_to(column, (64, 256)), 0.0), axis=0, keepdims=True)
    rows = lax.broadcasted_iota(jnp.int32, (32, 256), 0) + w * 32
    mine = rows == lax.broadcasted_iota(jnp.int32, (32, 256), 1)
    weight = jnp.sum(jnp.where(mine, jnp.broadcast_to(picked, (32, 256)), 0.0), axis=1, keepdims=True)
    weight = weight.astype(BF16).astype(F32)
    raw[3].wait()
    g_own[...] = (g_raw[...].astype(F32) * weight).astype(BF16).reshape(2, 16, 1536)

    pl.semaphore_wait(bar, 10 - c + z)

    @pl.when(c == 0)
    def _():
        pl.semaphore_signal(pin_sem, inc=1, device_id=partner, device_id_type=MESH)

    for d in range(1, NZ):

        @pl.when(z + d >= NZ)
        def _():
            pl.semaphore_signal(in_sem, inc=1, device_id=zdev(d), device_id_type=MESH)

    def xa_copy(n, dk, dy):
        to = lax.rem(k + dk, NK)
        return pltpu.make_async_remote_copy(
            src_ref=x_in.at[:, pl.ds(pl.multiple_of(to * 384, 384), 384)],
            dst_ref=xbuf.at[k, yl, zq, c, zh],
            send_sem=xa_s.at[n], recv_sem=xa_r.at[n], device_id=ydev(dk, dy), device_id_type=MESH,
        )

    def xa_wait():
        for n, (dk, dy) in enumerate(y_peers):
            frm = lax.rem(k + NK - dk, NK)
            arrived(xbuf.at[frm, 1 - yl if dy else yl, zq, c, zh], xa_s.at[n], xa_r.at[n], partner)

    def ye_send(d):
        send(g_own, gbuf.at[k, w, c], ye_s.at[d - 1], ye_r.at[d - 1], kdev(d))

    def ye_wait(d):
        frm = lax.rem(k + NK - d, NK)
        arrived(gbuf.at[frm, w, c], ye_s.at[d - 1], ye_r.at[d - 1], kdev(d))

    def away(e, s):
        return lax.rem(w - e * s + NX, NX)

    def pieces(p, e, s, cc):
        ref = gbuf.at[kp[p], away(e, s), cc]
        if p in (1, 2):
            return [(0, ref)] if s < HALF else []
        if s < HALF:
            return [(0, ref.at[0]), (1, ref.at[1])]
        j = 0 if e == 1 else 1
        return [(j, ref.at[j])]

    def ring_start(p):
        own = gbuf.at[kp[p], w, c]
        for j in (0,) if p in (1, 2) else (0, 1):
            for i, e in enumerate((1, -1)):
                dst = own if p in (1, 2) else own.at[j]
                src = g_own.at[j] if p == 0 else dst
                send(src, dst, ring_s.at[p, i, 0, j], ring_r.at[p, i, 0, j], xdev(e))

    def ring_adv(p, s):
        for n in (0, 1):
            for i, e in enumerate((1, -1)):
                here = pieces(p, e, s, c)
                if n >= len(here):
                    continue
                j, ref = here[n]
                arrived(ref, ring_s.at[p, i, s - 1, j], ring_r.at[p, i, s - 1, j], xdev(e))
                if s < HALF and j in [q for q, _ in pieces(p, e, s + 1, c)]:
                    send(ref, ref, ring_s.at[p, i, s, j], ring_r.at[p, i, s, j], xdev(e))

    def anti_send():
        ref = gbuf.at[k, away(1, HALF), c]
        for n, d in enumerate((1, 3)):
            send(ref, ref, an_s.at[n], an_r.at[n], kdev(d))

    def anti_wait(p):
        n = 1 if p == 1 else 0
        arrived(gbuf.at[kp[p], away(1, HALF), c], an_s.at[n], an_r.at[n], partner)

    def cc_send(p):
        ref = gbuf.at[kp[p], :, c]
        send(ref, ref, co_s.at[p], co_r.at[p], partner)

    def cc_last(n, e, s):
        ref = gbuf.at[kp[3], away(e, s), c]
        send(ref, ref, cc_s.at[n], cc_r.at[n], partner)

    def cc_wait(p):
        if p < 3:
            arrived(gbuf.at[kp[p], :, 1 - c], co_s.at[p], co_r.at[p], partner)
            return
        for n in range(NX):
            e, s = (1, n) if n <= HALF else (-1, n - HALF)
            arrived(gbuf.at[kp[3], away(e, s), 1 - c], cc_s.at[n], cc_r.at[n], partner)

    def z_send(above):
        ref = xbuf.at[:, :, zq, c, zh]
        for d in (4, 3, 5, 2, 6, 1, 7):

            @pl.when(z + d < NZ if above else z + d >= NZ)
            def _():
                pltpu.make_async_remote_copy(
                    src_ref=ref, dst_ref=ref, send_sem=zr_s.at[d], recv_sem=zr_r.at[d],
                    device_id=zdev(d), device_id_type=MESH,
                ).start()

    def z_wait():
        for d in range(1, NZ):
            zz = lax.rem(z + NZ - d, NZ)
            arrived(xbuf.at[:, :, zz // 2, c, lax.rem(zz, 2)], zr_s.at[d], zr_r.at[d], zdev(d))

    def z_sent():
        ref = xbuf.at[:, :, zq, c, zh]
        for d in range(1, NZ):
            pltpu.make_async_remote_copy(
                src_ref=ref, dst_ref=ref, send_sem=zr_s.at[d], recv_sem=zr_r.at[d],
                device_id=zdev(d), device_id_type=MESH,
            ).wait_send()

    def t3_dot(n):
        lhs = gbuf[k, :, c].reshape(256, 1536)
        out = lax.dot_general(
            lhs, wv[pl.ds(n * 512, 512), :], (((1,), (1,)), ((), ())), preferred_element_type=F32
        )
        part[:, :, :, pl.ds(n * 512, 512)] = out.astype(BF16).reshape(2, NZ, 16, 512)

    order = (4, 3, 5, 2, 6, 1, 7, 0)

    def t3_send():
        for d in order:
            zz = lax.rem(z + d, NZ)
            send(part.at[1 - yl, zz], rb1.at[d], t1_s.at[d], t1_r.at[d], yldev)

    def t3_pair(d):
        zz = lax.rem(z + d, NZ)
        arrived(rb1.at[d], t1_s.at[d], t1_r.at[d], yldev)
        both = part[yl, zz].astype(F32) + rb1[d].astype(F32)
        sb[d] = both.astype(BF16)

    def t3_out(d):
        if d:
            send(sb.at[d], rb2.at[d], t2_s.at[d], t2_r.at[d], zdev(d))

    def t3_final():
        total = sb[0].astype(F32)
        for d in range(1, NZ):
            arrived(rb2.at[d], t2_s.at[d], t2_r.at[d], zdev(d))
            total = total + rb2[d].astype(F32)
        gi_out[...] = total.astype(BF16)

    win = pl.ds(pl.multiple_of(c * 128, 128), 256)
    owin = pl.ds(pl.multiple_of((1 - c) * 128, 128), 256)

    def xc_send():
        ref = xbuf.at[:, :, :, c, :, :, owin]
        send(ref, ref, xc_s, xc_r, partner)

    def xc_wait():
        ref = xbuf.at[:, :, :, 1 - c, :, :, win]
        arrived(ref, xc_s, xc_r, partner)

    def t4(p):
        xt[...] = xbuf[kp[p], :, :, :, :, :, win].reshape(512, 256).T

        def step(n, _):
            col = pl.ds(pl.multiple_of(n * 512, 512), 512)
            rhs = gbuf[kp[p], :, :, :, :, col].reshape(512, 512)
            out = jnp.dot(xt[...], rhs, preferred_element_type=F32)
            if p == 0:
                acc[:, col] = out
            elif p < 3:
                acc[:, col] += out
            else:

                @pl.when(c == 0)
                def _():
                    gw_out[:, col] = acc[pl.ds(0, 192), col] + out[:192]

                @pl.when(c == 1)
                def _():
                    gw_out[:, col] = acc[pl.ds(64, 192), col] + out[64:]

            return 0

        lax.fori_loop(0, 3, step, 0)

    late = []

    def t3_next(count):
        for _ in range(count):
            d = order[len(late)]
            t3_pair(d)
            if late:
                t3_out(late[-1])
            late.append(d)

    ring_start(0)
    for n, at in enumerate(y_peers):
        cp = xa_copy(n, *at)
        cp.start()
        sends.append(cp)
    ye_send(1)
    ye_send(3)
    ye_send(2)
    keep = pltpu.make_async_copy(g_own, gbuf.at[k, w, c], loc_sem.at[0])
    keep.start()
    ring_adv(0, 1)
    ring_adv(0, 2)
    ye_wait(3)
    ring_start(1)
    loads[0].wait()
    xa_wait()
    z_send(False)
    ring_adv(0, 3)
    ye_wait(1)
    ring_start(2)
    ring_adv(0, 4)
    ye_wait(2)
    ring_start(3)
    keep.wait()
    loads[1].wait()
    t3_dot(0)
    t3_dot(1)
    ring_adv(1, 1)
    t3_dot(2)
    t3_send()
    anti_send()
    ring_adv(2, 1)

    @pl.when(z < NZ - 1)
    def _():
        pl.semaphore_wait(in_sem, NZ - 1 - z)

    z_send(True)
    ring_adv(1, 2)
    t3_next(1)
    ring_adv(3, 1)
    t3_next(2)
    ring_adv(2, 2)
    t3_next(2)
    ring_adv(3, 2)

    @pl.when(c == 1)
    def _():
        pl.semaphore_wait(pin_sem, 1)

    cc_send(0)
    cc_last(0, 1, 0)
    cc_last(1, 1, 1)
    cc_last(5, -1, 1)
    cc_last(2, 1, 2)
    cc_last(6, -1, 2)
    t3_next(3)
    ring_adv(1, 3)
    anti_wait(1)
    cc_send(1)
    ring_adv(2, 3)
    ring_adv(3, 3)
    z_wait()
    xc_send()
    anti_wait(2)
    cc_send(2)
    cc_last(3, 1, 3)
    cc_last(7, -1, 3)
    xc_wait()
    cc_wait(0)
    t4(0)
    cc_wait(1)
    t4(1)
    ring_adv(3, 4)
    cc_last(4, 1, 4)
    cc_wait(2)
    t4(2)
    cc_wait(3)
    t4(3)
    t3_final()
    z_sent()
    for cp in sends:
        cp.wait_send()


def body(saved_input, grad_out, weight, samples, correct, prompt_ids):
    dma = pltpu.SemaphoreType.DMA
    vm = pl.BlockSpec(memory_space=pltpu.VMEM)
    hbm = pl.BlockSpec(memory_space=pl.ANY)
    gw, gi = pl.pallas_call(
        kernel,
        out_shape=(
            pltpu.VMEM((192, 1536), F32),
            pltpu.VMEM((16, 1536), BF16),
        ),
        in_specs=[hbm] * 6,
        out_specs=(vm, vm),
        scratch_shapes=[
            pltpu.VMEM((1, 64), jnp.int32),
            pltpu.VMEM((1, 64), jnp.int32),
            pltpu.VMEM((1, 256), jnp.int32),
            pltpu.VMEM((32, 1536), BF16),
            pltpu.VMEM((2, 16, 1536), BF16),
            pltpu.VMEM((NK, NX, 2, 2, 16, 1536), BF16),
            pltpu.VMEM((NK, 2, 4, 2, 2, 16, 384), BF16),
            pltpu.VMEM((1536, 1536), BF16),
            pltpu.VMEM((2, NZ, 16, 1536), BF16),
            pltpu.VMEM((NZ, 16, 1536), BF16),
            pltpu.VMEM((NZ, 16, 1536), BF16),
            pltpu.VMEM((NZ, 16, 1536), BF16),
            pltpu.VMEM((256, 1536), F32),
            pltpu.VMEM((256, 512), BF16),
            dma((7,)),
            dma((4, 2, HALF, 2)), dma((4, 2, HALF, 2)),
            dma((3,)), dma((3,)),
            dma((NX,)), dma((NX,)),
            dma((3,)), dma((3,)),
            dma((7,)), dma((7,)),
            dma((2,)), dma((2,)),
            dma((NZ,)), dma((NZ,)),
            dma, dma,
            dma((NZ,)), dma((NZ,)),
            dma((NZ,)), dma((NZ,)),
            pltpu.SemaphoreType.REGULAR,
            pltpu.SemaphoreType.REGULAR,
        ],
        compiler_params=pltpu.CompilerParams(
            collective_id=0, has_side_effects=True, vmem_limit_bytes=56 * 1024 * 1024
        ),
        cost_estimate=pl.CostEstimate(flops=3_000_000_000, bytes_accessed=8_000_000, transcendentals=0),
    )(grad_out, saved_input, weight, samples[None, :], correct[None, :], prompt_ids[None, :])
    return gi, gw


def solution(mesh):
    in_specs = (
        P(("replica", "hidden"), "width"),
        P(("replica", "width"), "hidden"),
        P("width", "hidden"),
        P(),
        P(),
        P("replica"),
    )
    out_specs = (P(("replica", "hidden"), "width"), P(("width", "replica"), "hidden"))
    return jax.shard_map(body, mesh=mesh, in_specs=in_specs, out_specs=out_specs, check_vma=False)
```
